32 devices in a mesh: rep: 2 (over x), exp: 4 (over z), ten: 4 (over y, core).
Axes of the slice: x: 2, y: 2, z: 4, core: 2. Of those that a mesh axis runs over, the one named last changes fastest.
Arguments:
- hidden_in: bfloat16 [768, 3072], P(('rep', 'exp', 'ten')), parts along dimension 0, may hold values from -6 to 6
- queries: bfloat16 [768, 6144], P(('rep', 'exp', 'ten')), parts along dimension 0, may hold values from -100 to 100
- new_kv: bfloat16 [2, 768, 1024], P(None, ('rep', 'exp', 'ten')), parts along dimension 1, may hold values from -5 to 5
- prefix_kv: bfloat16 [2, 8, 128, 1024], P(None, ('rep', 'exp'), 'ten'), parts along dimension 1, may hold values from -5 to 5
- decode_kv: bfloat16 [2, 128, 48, 1024], P(None, ('rep', 'exp', 'ten')), parts along dimension 1, may hold values from -5 to 5
- prefix_len: int32 [8], P(('rep', 'exp')), parts along dimension 0, may hold values from 2 to 128
- decode_len: int32 [128], P(('rep', 'exp', 'ten')), parts along dimension 0, may hold values from 2 to 48
- out_proj: bfloat16 [6144, 3072], P('ten'), may hold values from -0.078125 to 0.078125
- norm_gain: float32 [3072], replicated, may hold values from 0.5 to 1.5
- router_w: bfloat16 [3072, 8], replicated, may hold values from -0.109375 to 0.109375
- expert_ids: int32 [768, 2], P(('rep', 'exp', 'ten')), parts along dimension 0, may hold values from 0 to 7, all different within a row; in each aligned block of 24 rows (0 to 23, 24 to 47, ...) at most 7 rows name the same one
- w_gate: bfloat16 [8, 3072, 8192], P('exp', None, 'ten'), may hold values from -0.109375 to 0.109375
- w_up: bfloat16 [8, 3072, 8192], P('exp', None, 'ten'), may hold values from -0.109375 to 0.109375
- w_down: bfloat16 [8, 8192, 3072], P('exp', 'ten'), may hold values from -0.0625 to 0.0625
Outputs:
- layer_out: bfloat16 [768, 3072], P(('rep', 'exp', 'ten')), parts along dimension 0
The draws below stay inside these ranges and needn't reach their ends.
There are 2 independent parts, one for each index of `rep`. The reference program is written for one: setup_inputs(seed, part) draws one part's arguments, and reference() takes and returns one part's arrays. A program takes and returns all parts, laid end to end along the dimension named above; an argument that names none is the same for every part. Nothing has to cross between parts.
Inputs may be any that keep to these rules, and one draw needn't show every extreme that they name: `expert_ids`: each row names two different experts. Within each aligned block of 24 rows (the rows of one device) no expert is named by more than 7 rows, and in some block one expert is named by exactly 7 rows.
All inputs are finite; a program needn't handle non-finite values.
Results may differ from the reference program's by a relative error of at most 0.013.
Values may be sent and summed in bfloat16 or wider, within the bound.
A program may use at most 128 MiB of HBM per device.

```python
import math
import jax
import jax.numpy as jnp
import numpy as np
from jax import lax

D = 3072
FF = 8192
HQ = 48
KVH = 8
HD = 128
EXPERTS = 8
ROWS_DEV = 24
DEC_DEV = 4
CTX_DEC = 48
CAP = 7
CH_DEV = 20
GROUP_ROWS = 96
SPAN = 80
DEC_GROUP = 16
TOKENS = 384
PREFIX = 128
DEC_ALL = 64
N_EXP = 4
N_TEN = 4


def joint_fields(key):
    base_key = jax.random.fold_in(key, 4417)
    key_query, key_prefix, key_decode = jax.random.split(base_key, 3)
    query_field = jnp.clip(jax.random.normal(key_query, (N_EXP, GROUP_ROWS, HQ, HD), jnp.float32), -5.0, 5.0)
    prefix_field = jnp.clip(jax.random.normal(key_prefix, (2, N_EXP, PREFIX, KVH, HD), jnp.float32), -5.0, 5.0)
    decode_field = jnp.clip(jax.random.normal(key_decode, (2, DEC_ALL, CTX_DEC, KVH, HD), jnp.float32), -5.0, 5.0)
    return (query_field, prefix_field, decode_field)


def draw_queries(key, part):
    return joint_fields(key)[0].reshape(TOKENS, HQ * HD).astype(jnp.bfloat16)


def draw_prefix_kv(key, part):
    return joint_fields(key)[1].reshape(2, N_EXP, PREFIX, KVH * HD).astype(jnp.bfloat16)


def draw_decode_kv(key, part):
    return joint_fields(key)[2].reshape(2, DEC_ALL, CTX_DEC, KVH * HD).astype(jnp.bfloat16)


def plant(entries, key, smallest, high):
    spot = [jax.random.randint(jax.random.fold_in(key, axis), (), 0, length) for axis, length in enumerate(entries.shape)]
    main_axis = entries.shape.index(max(entries.shape))
    neighbour = spot[:main_axis] + [(spot[main_axis] + 1) % entries.shape[main_axis]] + spot[main_axis + 1:]
    return entries.at[tuple(spot)].set(smallest).at[tuple(neighbour)].set(high)


def block_scale(stream_key, dims, cuts, smallest, top_value):
    factor_of = 1.0
    for position, blocks in cuts:
        steps = jax.random.uniform(jax.random.fold_in(jax.random.fold_in(stream_key, 6), position), (blocks,), jnp.float32, smallest / len(cuts), top_value / len(cuts))
        factor_of = factor_of * jnp.repeat(jnp.exp(steps), dims[position] // blocks).reshape((-1,) + (1,) * (len(dims) - 1 - position))
    return factor_of


def deal_out(key, own, number, rows, number_of, top, reach, skew):
    sequence = jax.random.permutation(key, number_of)
    packed, usual = load_shares(number_of, rows * top, reach, skew, True), load_shares(number_of, rows * top, reach, skew, False)
    places = jnp.arange(number_of)

    def named(sizes, offset_by):
        used = int((sizes > 0).sum())
        fixed = max(1, used // 4)
        shifted = fixed + (places - fixed + offset_by * (used - fixed)) % max(1, number_of - fixed)
        return jnp.zeros((number_of,), jnp.int32).at[sequence[jnp.where(places < fixed, places, shifted)]].set(jnp.asarray(sizes, jnp.int32))

    sizes = jnp.where(number % 4 == 0, named(packed, number // 4), named(usual, number - number // 4 - 1))
    mixed = jax.random.permutation(jax.random.fold_in(own, 3), number_of)
    giver, receiver = mixed[0:number_of // 2 * 2:2], mixed[1:number_of // 2 * 2:2]
    slack = jnp.minimum(sizes[giver] - 1, reach - sizes[receiver]) // 2
    slack = jnp.where((giver == sequence[0]) | (receiver == sequence[0]) | (sizes[receiver] == 0), 0, jnp.maximum(slack, 0))
    shifted = jax.random.randint(jax.random.fold_in(own, 4), (number_of // 2,), 0, 1 << 20) % (slack + 1)
    sizes = sizes.at[giver].add(-shifted).at[receiver].add(shifted)
    items = jnp.searchsorted(jnp.cumsum(sizes), jnp.arange(rows * top), side="right").astype(jnp.int32)
    grid = items.reshape(top, rows).T
    grid = grid[jax.random.permutation(jax.random.fold_in(own, 1), rows)]
    offset_by = jax.random.randint(jax.random.fold_in(own, 2), (rows, 1), 0, top)
    return jnp.take_along_axis(grid, (jnp.arange(top)[None, :] + offset_by) % top, axis=1)


def load_shares(number_of, total, reach, slope, full):
    portions = [(1 << 20) // math.isqrt(grade ** slope) + 1 for grade in range(1, number_of + 1)]
    largest = reach if full else min(reach, max(-(-total // number_of), total * portions[0] // sum(portions)))
    least = 1 if total - largest >= number_of - 1 else 0
    given, surplus = [largest] + [least] * (number_of - 1), total - largest - least * (number_of - 1)
    while surplus > 0:
        free = [i for i in range(1, number_of) if given[i] < largest] or [i for i in range(1, number_of) if given[i] < reach]
        whole, left = sum([portions[i] for i in free]), surplus
        for i in free:
            more = min(reach - given[i], max(1, left * portions[i] // whole), surplus)
            given[i] = given[i] + more
            surplus = surplus - more
    return np.array(given)


def noise(stream_key, shape, deviation, bound, shards=(), kind=jnp.bfloat16):
    loudness = block_scale(stream_key, shape, shards, -0.22, 0.18) if shards else 1.0
    entries = jax.random.normal(stream_key, shape, jnp.float32) * deviation * loudness
    return jnp.minimum(jnp.maximum(entries, -bound), bound).astype(kind)


def setup_inputs(seed: int = 0, part: int = 0) -> dict:
    splits = jax.random.split(jax.random.key(seed), 15)
    part_keys = jax.random.split(jax.random.fold_in(splits[14], part), 15)
    hidden_in = noise(part_keys[0], (TOKENS, D), 1.0, 6.0, ((0, 16),))
    queries = draw_queries(jax.random.fold_in(jax.random.fold_in(splits[14], part), 71), part)
    new_kv = noise(part_keys[2], (2, TOKENS, KVH * HD), 1.0, 5.0, ((1, 16),))
    prefix_kv = draw_prefix_kv(jax.random.fold_in(jax.random.fold_in(splits[14], part), 71), part)
    decode_kv = draw_decode_kv(jax.random.fold_in(jax.random.fold_in(splits[14], part), 71), part)
    prefix_len = plant(jax.random.randint(part_keys[5], (N_EXP,), 2, PREFIX + 1), jax.random.fold_in(part_keys[5], 1), 2, PREFIX).astype(jnp.int32)
    decode_len = plant(jax.random.randint(part_keys[6], (DEC_ALL,), 2, CTX_DEC + 1), jax.random.fold_in(part_keys[6], 1), 2, CTX_DEC).astype(jnp.int32)
    out_proj = noise(splits[7], (HQ * HD, D), (HQ * HD) ** -0.5, 0.078125, ((0, 4),))
    norm_gain = jnp.clip(1.0 + 0.1 * jax.random.normal(splits[8], (D,), jnp.float32), 0.5, 1.5)
    router_w = noise(splits[9], (D, EXPERTS), D ** -0.5, 0.109375)
    expert_ids_keys = jax.random.split(jax.random.fold_in(part_keys[10], 1), TOKENS // ROWS_DEV)
    expert_ids_turns = jax.random.permutation(jax.random.fold_in(part_keys[10], 3), TOKENS // ROWS_DEV)
    expert_ids = jax.vmap(lambda own, number: deal_out(jax.random.fold_in(part_keys[10], 2), own, number, ROWS_DEV, EXPERTS, 2, CAP, 2))(expert_ids_keys, expert_ids_turns).reshape((TOKENS, 2))
    w_gate = noise(splits[11], (EXPERTS, D, FF), D ** -0.5, 0.109375, ((0, 4), (2, 4)))
    w_up = noise(splits[12], (EXPERTS, D, FF), D ** -0.5, 0.109375, ((0, 4), (2, 4)))
    w_down = noise(splits[13], (EXPERTS, FF, D), FF ** -0.5, 0.0625, ((0, 4), (1, 4)))
    return {"hidden_in": hidden_in, "queries": queries, "new_kv": new_kv, "prefix_kv": prefix_kv, "decode_kv": decode_kv, "prefix_len": prefix_len, "decode_len": decode_len, "out_proj": out_proj, "norm_gain": norm_gain, "router_w": router_w, "expert_ids": expert_ids, "w_gate": w_gate, "w_up": w_up, "w_down": w_down}


def attend(scores, visible, values, pattern):
    masked = jnp.where(visible, scores, -jnp.inf)
    row_max = lax.optimization_barrier(jnp.max(masked, axis=-1, keepdims=True))
    exponent = jnp.exp(masked - row_max)
    totals = lax.optimization_barrier(jnp.sum(exponent, axis=-1))
    weights = exponent.astype(jnp.bfloat16).astype(jnp.float32)
    return (jnp.einsum(pattern, weights, values) / totals[..., None]).astype(jnp.bfloat16)

def group_attention(group, queries, new_kv, prefix_kv, decode_kv, prefix_len, decode_len):
    per_kv = HQ // KVH
    score_scale = HD ** (-0.5)
    first_row = group * GROUP_ROWS
    query_rows = queries[first_row:first_row + GROUP_ROWS].astype(jnp.float32).reshape(N_TEN, ROWS_DEV, KVH, per_kv, HD)
    key_rows = new_kv[0, first_row:first_row + GROUP_ROWS].astype(jnp.float32).reshape(N_TEN, ROWS_DEV, KVH, HD)
    value_rows = new_kv[1, first_row:first_row + GROUP_ROWS].astype(jnp.float32).reshape(N_TEN, ROWS_DEV, KVH, HD)
    span_queries = query_rows[:, :CH_DEV].reshape(SPAN, KVH, per_kv, HD)
    span_keys = key_rows[:, :CH_DEV].reshape(SPAN, KVH, HD)
    span_values = value_rows[:, :CH_DEV].reshape(SPAN, KVH, HD)
    prefill_keys = jnp.concatenate([prefix_kv[0, group].astype(jnp.float32).reshape(PREFIX, KVH, HD), span_keys], axis=0)
    prefill_values = jnp.concatenate([prefix_kv[1, group].astype(jnp.float32).reshape(PREFIX, KVH, HD), span_values], axis=0)
    scores = jnp.einsum('rcgh,pch->rcgp', span_queries, prefill_keys) * score_scale
    positions = jnp.arange(PREFIX + SPAN, dtype=jnp.int32)[None, :]
    row_index = jnp.arange(SPAN, dtype=jnp.int32)[:, None]
    visible = jnp.where(positions < PREFIX, positions < prefix_len[group], positions - PREFIX <= row_index)
    prefill_out = attend(scores, visible[:, None, None, :], prefill_values, 'rcgp,pch->rcgh')
    first_seq = group * DEC_GROUP
    dec_queries = query_rows[:, CH_DEV:].reshape(DEC_GROUP, KVH, per_kv, HD)
    own_keys = key_rows[:, CH_DEV:].reshape(DEC_GROUP, KVH, HD)
    own_values = value_rows[:, CH_DEV:].reshape(DEC_GROUP, KVH, HD)
    decode_keys = jnp.concatenate([decode_kv[0, first_seq:first_seq + DEC_GROUP].astype(jnp.float32).reshape(DEC_GROUP, CTX_DEC, KVH, HD), own_keys[:, None]], axis=1)
    decode_values = jnp.concatenate([decode_kv[1, first_seq:first_seq + DEC_GROUP].astype(jnp.float32).reshape(DEC_GROUP, CTX_DEC, KVH, HD), own_values[:, None]], axis=1)
    decode_scores = jnp.einsum('dcgh,dpch->dcgp', dec_queries, decode_keys) * score_scale
    decode_pos = jnp.arange(CTX_DEC + 1, dtype=jnp.int32)[None, :]
    lengths = decode_len[first_seq:first_seq + DEC_GROUP][:, None]
    visible_dec = (decode_pos < lengths) | (decode_pos == CTX_DEC)
    decode_out = attend(decode_scores, visible_dec[:, None, None, :], decode_values, 'dcgp,dpch->dcgh')
    combined = jnp.concatenate([prefill_out.reshape(N_TEN, CH_DEV, HQ * HD), decode_out.reshape(N_TEN, DEC_DEV, HQ * HD)], axis=1)
    return combined.reshape(GROUP_ROWS, HQ * HD)

def run_expert(bundle):
    slot_rows, gate_weight, up_weight, down_weight = bundle
    gate_act = jnp.dot(slot_rows, gate_weight, preferred_element_type=jnp.float32)
    up_act = jnp.dot(slot_rows, up_weight, preferred_element_type=jnp.float32)
    hidden = (jax.nn.silu(gate_act) * up_act).astype(jnp.bfloat16)
    return jnp.dot(hidden, down_weight, preferred_element_type=jnp.float32).astype(jnp.bfloat16)

def reference(hidden_in, queries, new_kv, prefix_kv, decode_kv, prefix_len, decode_len, out_proj, norm_gain, router_w, expert_ids, w_gate, w_up, w_down):
    pieces = []
    for group in range(N_EXP):
        pieces.append(group_attention(group, queries, new_kv, prefix_kv, decode_kv, prefix_len, decode_len))
    attended = jnp.concatenate(pieces, axis=0)
    residual = hidden_in.astype(jnp.float32) + jnp.dot(attended, out_proj, preferred_element_type=jnp.float32)
    mean_square = lax.optimization_barrier(jnp.mean(residual * residual, axis=1, keepdims=True))
    normed = (residual * lax.rsqrt(mean_square + 1e-05) * norm_gain).astype(jnp.bfloat16)
    logits = jnp.dot(normed, router_w, preferred_element_type=jnp.float32)
    chosen_logits = jnp.take_along_axis(logits, expert_ids, axis=1)
    route_weights = jax.nn.softmax(chosen_logits, axis=1)
    blocks = TOKENS // ROWS_DEV
    chosen = expert_ids.reshape(blocks, ROWS_DEV * 2)
    chosen_hot = (chosen[:, :, None] == jnp.arange(EXPERTS, dtype=jnp.int32)).astype(jnp.int32)
    earlier = jnp.cumsum(chosen_hot, axis=1) - chosen_hot
    slot_rank = lax.optimization_barrier(jnp.sum(earlier * chosen_hot, axis=2))
    slot_flat = (jnp.arange(blocks, dtype=jnp.int32)[:, None] * CAP + slot_rank).reshape(-1).astype(jnp.int32)
    expert_flat = expert_ids.reshape(-1).astype(jnp.int32)
    token_of = jnp.repeat(jnp.arange(TOKENS, dtype=jnp.int32), 2)
    buffer = jnp.zeros((EXPERTS, blocks * CAP, D), jnp.bfloat16).at[expert_flat, slot_flat].set(normed[token_of])
    expert_out = lax.map(run_expert, (buffer, w_gate, w_up, w_down))
    picked = expert_out[expert_flat, slot_flat].reshape(TOKENS, 2, D).astype(jnp.float32)
    mixed = residual + route_weights[:, 0:1] * picked[:, 0] + route_weights[:, 1:2] * picked[:, 1]
    return mixed.astype(jnp.bfloat16)
```

```python
import jax
import jax.numpy as jnp
from jax import lax
from jax.experimental import pallas as pl
from jax.experimental.pallas import tpu as pltpu
from jax.sharding import PartitionSpec as P

HD = 128


lowest_score = -1e30


def local_softmax(scores, visible):
    masked = jnp.where(visible, scores, lowest_score)
    row_max = jnp.max(masked, axis=-1)
    exponent = jnp.where(visible, jnp.exp(masked - row_max[..., None]), 0.0)
    return (row_max, exponent, jnp.sum(exponent, axis=-1))


MESH = pl.DeviceIdType.MESH
VMEM = pl.BlockSpec(memory_space=pltpu.VMEM)
SLOTS = 8
VMEM_LIMIT = 60 * 1024 * 1024


def greet(peers):
    sem = pltpu.get_barrier_semaphore()
    for peer in peers:
        pl.semaphore_signal(sem, inc=1, device_id=peer, device_id_type=MESH)
    pl.semaphore_wait(sem, len(peers))


def send(src, dst, send_sem, recv_sem, peer):
    copy = pltpu.make_async_remote_copy(
        src_ref=src,
        dst_ref=dst,
        send_sem=send_sem,
        recv_sem=recv_sem,
        device_id=peer,
        device_id_type=MESH,
    )
    copy.start()
    return copy


def call(kernel, out_shape, scratch, collective_id, args, out_specs=None):
    return pl.pallas_call(
        kernel,
        out_shape=out_shape,
        in_specs=[VMEM] * len(args),
        out_specs=jax.tree.map(lambda _: VMEM, out_shape),
        scratch_shapes=scratch,
        compiler_params=pltpu.CompilerParams(
            collective_id=collective_id, has_side_effects=True, vmem_limit_bytes=VMEM_LIMIT
        ),
    )(*args)


def coords():
    t = lax.axis_index("ten")
    return t, t // 2, lax.rem(t, 2)


def gather_ten(arrays, collective_id):
    ten = lax.axis_size("ten")
    chips = ten // 2
    count = len(arrays)

    def kernel(*refs):
        ins, outs = refs[:count], refs[count : 2 * count]
        far_s, far_r, core_s, core_r, local = refs[2 * count :]
        t, y, c = coords()
        partner = {"ten": y * 2 + 1 - c}
        far = [{"ten": lax.rem(y + k, chips) * 2 + c} for k in range(1, chips)]
        greet(far + [partner])
        copies, own = [], []
        for k in range(1, chips):
            copies.append(
                [
                    send(ins[i], outs[i].at[t], far_s.at[i, k], far_r.at[i, k], far[k - 1])
                    for i in range(count)
                ]
            )
        core = []
        for i in range(count):
            core.append(send(ins[i], outs[i].at[t], core_s.at[i, 0], core_r.at[i, 0], partner))
            mine = pltpu.make_async_copy(ins[i], outs[i].at[t], local.at[i])
            mine.start()
            own.append(mine)
        for k in range(1, chips):
            origin = lax.rem(y - k + chips, chips) * 2 + c
            for i in range(count):
                copies[k - 1][i].wait_recv()
                block = outs[i].at[origin]
                core.append(send(block, block, core_s.at[i, k], core_r.at[i, k], partner))
        for row in copies:
            for copy in row:
                copy.wait_send()
        for copy in core:
            copy.wait()
        for copy in own:
            copy.wait()

    dma = pltpu.SemaphoreType.DMA
    return call(
        kernel,
        [jax.ShapeDtypeStruct((ten,) + a.shape, a.dtype) for a in arrays],
        [dma((count, chips))] * 4 + [dma((count,))],
        collective_id,
        arrays,
    )


def swap_columns(x, collective_id):
    ten = lax.axis_size("ten")
    rows, columns = x.shape
    width = columns // ten

    def kernel(x_ref, o_ref, s_sem, r_sem, local):
        t = lax.axis_index("ten")
        peers = [lax.rem(t + k, ten) for k in range(1, ten)]
        greet([{"ten": p} for p in peers])

        def part(p):
            return x_ref.at[:, pl.ds(pl.multiple_of(p * width, 128), width)]

        copies = [
            send(part(p), o_ref.at[t], s_sem.at[k], r_sem.at[k], {"ten": p})
            for k, p in enumerate(peers)
        ]
        own = pltpu.make_async_copy(part(t), o_ref.at[t], local)
        own.start()
        own.wait()
        for copy in copies:
            copy.wait()

    dma = pltpu.SemaphoreType.DMA
    return call(
        kernel,
        jax.ShapeDtypeStruct((ten, rows, width), x.dtype),
        [dma((ten - 1,)), dma((ten - 1,)), dma],
        collective_id,
        [x],
    )


def scatter_sum(x, collective_id):
    ten, rows, columns = x.shape
    chips = ten // 2

    def kernel(x_ref, o_ref, near, pair, landed, core_s, core_r, far_s, far_r):
        t, y, c = coords()
        partner = {"ten": y * 2 + 1 - c}
        order = [lax.rem(y + k, chips) for k in range(chips)]
        greet([{"ten": order[k] * 2 + c} for k in range(1, chips)] + [partner])
        sequence = list(range(1, chips)) + [0]
        core = {}
        for k in sequence:
            core[k] = send(
                x_ref.at[order[k] * 2 + 1 - c], near.at[k], core_s.at[k], core_r.at[k], partner
            )
        far = []
        for k in sequence:
            core[k].wait_recv()
            total = x_ref[order[k] * 2 + c].astype(jnp.float32) + near[k].astype(jnp.float32)
            if k:
                pair[k] = total.astype(pair.dtype)
                far.append(
                    send(
                        pair.at[k],
                        landed.at[k],
                        far_s.at[k],
                        far_r.at[k],
                        {"ten": order[k] * 2 + c},
                    )
                )
            else:
                o_ref[...] = total
        for k, copy in enumerate(far, 1):
            copy.wait_recv()
            o_ref[...] += landed[k].astype(jnp.float32)
        for copy in far + list(core.values()):
            copy.wait_send()

    dma = pltpu.SemaphoreType.DMA
    buffer = pltpu.VMEM((chips, rows, columns), x.dtype)
    return call(
        kernel,
        jax.ShapeDtypeStruct((rows, columns), jnp.float32),
        [buffer] * 3 + [dma((chips,))] * 4,
        collective_id,
        [x],
    )


def dispatch(x, collective_id):
    groups, slots, width = x.shape
    ten = lax.axis_size("ten")
    chips = ten // 2

    def kernel(x_ref, o_ref, z_s, z_r, y_s, y_r, c_s, c_r, local):
        t, y, c = coords()
        g = lax.axis_index("exp")
        partner = {"ten": y * 2 + 1 - c}
        order = [lax.rem(g + k, groups) for k in range(groups)]
        far = [{"ten": lax.rem(y + j, chips) * 2 + c} for j in range(1, chips)]
        greet([{"exp": order[k]} for k in range(1, groups)] + far + [partner])
        across = [
            send(x_ref.at[order[k]], o_ref.at[t, g], z_s.at[k], z_r.at[k], {"exp": order[k]})
            for k in range(1, groups)
        ]
        mine = pltpu.make_async_copy(x_ref.at[g], o_ref.at[t, g], local)
        mine.start()
        far_copies, core = {}, []
        for k in range(groups):
            origin = lax.rem(g - k + groups, groups)
            block = o_ref.at[t, origin]
            if k:
                across[k - 1].wait_recv()
            source = block if k else x_ref.at[g]
            for j in range(1, chips):
                far_copies[k, j] = send(
                    source, block, y_s.at[k, j], y_r.at[k, j], far[j - 1]
                )
            core.append(send(source, block, c_s.at[k, 0], c_r.at[k, 0], partner))
        for k in range(groups):
            origin = lax.rem(g - k + groups, groups)
            for j in range(1, chips):
                far_copies[k, j].wait_recv()
                block = o_ref.at[lax.rem(y - j + chips, chips) * 2 + c, origin]
                core.append(send(block, block, c_s.at[k, j], c_r.at[k, j], partner))
        for copy in across + list(far_copies.values()):
            copy.wait_send()
        mine.wait()
        for copy in core:
            copy.wait()

    dma = pltpu.SemaphoreType.DMA
    return call(
        kernel,
        jax.ShapeDtypeStruct((ten, groups, slots, width), x.dtype),
        [dma((groups,))] * 2 + [dma((groups, chips))] * 4 + [dma],
        collective_id,
        [x],
    )


def collect(x, collective_id):
    ten, groups, slots, width = x.shape
    chips = ten // 2

    def kernel(x_ref, o_ref, near, pair, landed, ready, c_s, c_r, y_s, y_r, z_s, z_r):
        t, y, c = coords()
        g = lax.axis_index("exp")
        partner = {"ten": y * 2 + 1 - c}
        order = [lax.rem(g + k, groups) for k in range(groups)]
        rows = [lax.rem(y + j, chips) for j in range(chips)]
        far = [{"ten": rows[j] * 2 + c} for j in range(1, chips)]
        greet([{"exp": order[k]} for k in range(1, groups)] + far + [partner])
        sequence = list(range(1, groups)) + [0]
        inner = list(range(1, chips)) + [0]
        core, out = {}, {}
        for k in sequence:
            for j in inner:
                core[k, j] = send(
                    x_ref.at[rows[j] * 2 + 1 - c, order[k]],
                    near.at[k, j],
                    c_s.at[k, j],
                    c_r.at[k, j],
                    partner,
                )

        def summed(k, j):
            core[k, j].wait_recv()
            block = x_ref[rows[j] * 2 + c, order[k]]
            return block.astype(jnp.float32) + near[k, j].astype(jnp.float32)

        for k in sequence:
            for j in range(1, chips):
                pair[k, j] = summed(k, j).astype(pair.dtype)
                out[k, j] = send(
                    pair.at[k, j], landed.at[k, j], y_s.at[k, j], y_r.at[k, j], far[j - 1]
                )
        back = []
        for k in sequence:
            total = summed(k, 0)
            for j in range(1, chips):
                out[k, j].wait_recv()
                total = total + landed[k, j].astype(jnp.float32)
            if k:
                ready[k] = total.astype(ready.dtype)
                back.append(
                    send(
                        ready.at[k], o_ref.at[g], z_s.at[k], z_r.at[k], {"exp": order[k]}
                    )
                )
            else:
                o_ref[g] = total.astype(o_ref.dtype)
        for copy in list(core.values()) + list(out.values()):
            copy.wait_send()
        for copy in back:
            copy.wait()

    dma = pltpu.SemaphoreType.DMA
    buffer = pltpu.VMEM((groups, chips, slots, width), x.dtype)
    return call(
        kernel,
        jax.ShapeDtypeStruct((groups, slots, width), x.dtype),
        [buffer] * 3
        + [pltpu.VMEM((groups, slots, width), x.dtype)]
        + [dma((groups, chips))] * 4
        + [dma((groups,))] * 2,
        collective_id,
        [x],
    )


def on_device(
    hidden_in,
    queries,
    new_kv,
    prefix_kv,
    decode_kv,
    prefix_len,
    decode_len,
    out_proj,
    norm_gain,
    router_w,
    expert_ids,
    w_gate,
    w_up,
    w_down,
):
    ten_size = lax.axis_size("ten")
    groups = lax.axis_size("exp")
    my_ten = lax.axis_index("ten")
    rows_dev, model_width = hidden_in.shape
    dec_dev = decode_len.shape[0]
    span_dev = rows_dev - dec_dev
    span_rows = span_dev * ten_size
    kv_width = new_kv.shape[2]
    heads_kv = kv_width // HD
    heads_q = queries.shape[1] // HD
    per_kv = heads_q // heads_kv
    score_scale = HD ** (-0.5)
    ctx_len = decode_kv.shape[2]
    own_heads = queries.reshape(rows_dev, heads_kv, per_kv, HD)
    dec_keys = jnp.concatenate([decode_kv[0], new_kv[0, span_dev:, None]], axis=1).reshape(
        dec_dev, ctx_len + 1, heads_kv, HD
    )
    dec_values = jnp.concatenate([decode_kv[1], new_kv[1, span_dev:, None]], axis=1).reshape(
        dec_dev, ctx_len + 1, heads_kv, HD
    )
    dec_scores = (
        jnp.einsum(
            "dcgh,dpch->dcgp", own_heads[span_dev:], dec_keys, preferred_element_type=jnp.float32
        )
        * score_scale
    )
    dec_pos = jnp.arange(ctx_len + 1, dtype=jnp.int32)[None, :]
    dec_visible = ((dec_pos < decode_len[:, None]) | (dec_pos == ctx_len))[:, None, None, :]
    dec_max, dec_exponent, dec_totals = local_softmax(dec_scores, dec_visible)
    dec_partial = jnp.einsum(
        "dcgp,dpch->dcgh",
        dec_exponent.astype(jnp.bfloat16),
        dec_values,
        preferred_element_type=jnp.float32,
    )
    parts = gather_ten([prefix_kv[0, 0], prefix_kv[1, 0], new_kv[0, :span_dev], new_kv[1, :span_dev]], 0)
    parts = [p.reshape(-1, kv_width) for p in parts]
    full_prefix, full_fresh = parts[:2], parts[2:]
    prefix_total = full_prefix[0].shape[0]
    key_rows = jnp.concatenate([full_prefix[0], full_fresh[0]], axis=0).reshape(
        prefix_total + span_rows, heads_kv, HD
    )
    value_rows = jnp.concatenate([full_prefix[1], full_fresh[1]], axis=0).reshape(
        prefix_total + span_rows, heads_kv, HD
    )
    scores = (
        jnp.einsum(
            "rcgh,pch->rcgp", own_heads[:span_dev], key_rows, preferred_element_type=jnp.float32
        )
        * score_scale
    )
    query_row = my_ten * span_dev + jnp.arange(span_dev, dtype=jnp.int32)[:, None]
    positions = jnp.arange(prefix_total + span_rows, dtype=jnp.int32)[None, :]
    visible = jnp.where(
        positions < prefix_total, positions < prefix_len[0], positions - prefix_total <= query_row
    )[:, None, None, :]
    row_max, exponent, totals = local_softmax(scores, visible)
    span_out = (
        jnp.einsum(
            "rcgp,pch->rcgh",
            exponent.astype(jnp.bfloat16),
            value_rows,
            preferred_element_type=jnp.float32,
        )
        / totals[..., None]
    )
    dec_out = dec_partial / dec_totals[..., None]
    attended_rows = (
        jnp.concatenate([span_out, dec_out], axis=0)
        .reshape(rows_dev, heads_q * HD)
        .astype(jnp.bfloat16)
    )
    row_block = swap_columns(attended_rows, 1).reshape(ten_size * rows_dev, -1)
    shares = jnp.dot(row_block, out_proj, preferred_element_type=jnp.float32).astype(jnp.bfloat16)
    projected = scatter_sum(shares.reshape(ten_size, rows_dev, model_width), 2)
    residual = hidden_in.astype(jnp.float32) + projected
    mean_square = jnp.mean(residual * residual, axis=1, keepdims=True)
    normed = (residual * lax.rsqrt(mean_square + 1e-05) * norm_gain).astype(jnp.bfloat16)
    logits = jnp.dot(normed, router_w, preferred_element_type=jnp.float32)
    experts = router_w.shape[1]
    chosen_hot = (expert_ids[:, :, None] == jnp.arange(experts, dtype=jnp.int32)).astype(jnp.int32)
    chosen_logits = jnp.sum(jnp.where(chosen_hot == 1, logits[:, None, :], 0.0), axis=2)
    route_weights = jax.nn.softmax(chosen_logits, axis=1)
    flat_hot = chosen_hot.reshape(rows_dev * 2, experts)
    slot_rank = jnp.sum((jnp.cumsum(flat_hot, axis=0) - flat_hot) * flat_hot, axis=1).reshape(
        rows_dev, 2
    )
    capacity = SLOTS
    slot_index = jnp.arange(capacity, dtype=jnp.int32)
    assignment = chosen_hot[:, :, :, None] * (slot_rank[:, :, None, None] == slot_index).astype(
        jnp.int32
    )
    placement = jnp.sum(assignment, axis=1)
    local_experts = experts // groups
    placement_split = placement.reshape(rows_dev, groups, local_experts, capacity).astype(
        jnp.bfloat16
    )
    outgoing = jnp.einsum(
        "rnlc,rd->nlcd", placement_split, normed, preferred_element_type=jnp.float32
    ).astype(jnp.bfloat16)
    arrived = dispatch(outgoing.reshape(groups, local_experts * capacity, model_width), 3)
    shard_rows = arrived.reshape(ten_size * groups, local_experts, capacity, model_width)
    shard_rows = shard_rows.transpose(1, 0, 2, 3).reshape(local_experts, -1, model_width)
    gate_act = jnp.einsum("lsd,ldf->lsf", shard_rows, w_gate, preferred_element_type=jnp.float32)
    up_act = jnp.einsum("lsd,ldf->lsf", shard_rows, w_up, preferred_element_type=jnp.float32)
    hidden = (jax.nn.silu(gate_act) * up_act).astype(jnp.bfloat16)
    down = jnp.einsum("lsf,lfd->lsd", hidden, w_down, preferred_element_type=jnp.float32)
    down = down.astype(jnp.bfloat16).reshape(local_experts, ten_size, groups, capacity, model_width)
    down = down.transpose(1, 2, 0, 3, 4)
    returned = collect(down.reshape(ten_size, groups, local_experts * capacity, model_width), 4)
    outputs = returned.reshape(experts * capacity, model_width).astype(jnp.float32)
    weight_map = jnp.sum(
        assignment.astype(jnp.float32) * route_weights[:, :, None, None], axis=1
    ).reshape(rows_dev, experts * capacity)
    expert_mix = jnp.dot(
        weight_map, outputs, precision=lax.Precision.HIGHEST, preferred_element_type=jnp.float32
    )
    return (residual + expert_mix).astype(jnp.bfloat16)


def solution(mesh):
    in_specs = (
        P(("rep", "exp", "ten"), None),
        P(("rep", "exp", "ten"), None),
        P(None, ("rep", "exp", "ten"), None),
        P(None, ("rep", "exp"), "ten", None),
        P(None, ("rep", "exp", "ten"), None, None),
        P(("rep", "exp")),
        P(("rep", "exp", "ten")),
        P("ten", None),
        P(),
        P(),
        P(("rep", "exp", "ten"), None),
        P("exp", None, "ten"),
        P("exp", None, "ten"),
        P("exp", "ten", None),
    )
    out_specs = P(("rep", "exp", "ten"), None)
    return jax.shard_map(
        on_device, mesh=mesh, in_specs=in_specs, out_specs=out_specs, check_vma=False
    )
```

```python
import jax
import jax.numpy as jnp
from jax import lax
from jax.experimental import pallas as pl
from jax.experimental.pallas import tpu as pltpu
from jax.sharding import PartitionSpec as P

HD = 128


lowest_score = -1e30


def local_softmax(scores, visible):
    masked = jnp.where(visible, scores, lowest_score)
    row_max = jnp.max(masked, axis=-1)
    exponent = jnp.where(visible, jnp.exp(masked - row_max[..., None]), 0.0)
    return (row_max, exponent, jnp.sum(exponent, axis=-1))


MESH = pl.DeviceIdType.MESH
VMEM = pl.BlockSpec(memory_space=pltpu.VMEM)
SLOTS = 8
VMEM_LIMIT = 60 * 1024 * 1024


def greet(peers):
    sem = pltpu.get_barrier_semaphore()
    for peer in peers:
        pl.semaphore_signal(sem, inc=1, device_id=peer, device_id_type=MESH)
    pl.semaphore_wait(sem, len(peers))


def send(src, dst, send_sem, recv_sem, peer):
    copy = pltpu.make_async_remote_copy(
        src_ref=src,
        dst_ref=dst,
        send_sem=send_sem,
        recv_sem=recv_sem,
        device_id=peer,
        device_id_type=MESH,
    )
    copy.start()
    return copy


def call(kernel, out_shape, scratch, collective_id, args, out_specs=None):
    return pl.pallas_call(
        kernel,
        out_shape=out_shape,
        in_specs=[VMEM] * len(args),
        out_specs=jax.tree.map(lambda _: VMEM, out_shape),
        scratch_shapes=scratch,
        compiler_params=pltpu.CompilerParams(
            collective_id=collective_id, has_side_effects=True, vmem_limit_bytes=VMEM_LIMIT
        ),
    )(*args)


def coords():
    t = lax.axis_index("ten")
    return t, t // 2, lax.rem(t, 2)


def gather_cache(prefix, fresh, collective_id):
    ten = lax.axis_size("ten")
    chips = ten // 2
    pair, cached, width = prefix.shape
    rows = cached + fresh.shape[1]

    def kernel(prefix_ref, fresh_ref, o_ref, far_s, far_r, core_s, core_r, local):
        t, y, c = coords()
        partner = {"ten": y * 2 + 1 - c}
        far = [{"ten": lax.rem(y + k, chips) * 2 + c} for k in range(1, chips)]
        greet(far + [partner])
        places = [
            (prefix_ref, o_ref.at[:, t, pl.ds(0, cached)]),
            (fresh_ref, o_ref.at[:, t, pl.ds(cached, rows - cached)]),
        ]
        far_copies = {}
        for k in range(1, chips):
            for i, (source, place) in enumerate(places):
                far_copies[k, i] = send(
                    source, place, far_s.at[k, i], far_r.at[k, i], far[k - 1]
                )
        core, own = [], []
        for i, (source, place) in enumerate(places):
            core.append(send(source, place, core_s.at[0, i], core_r.at[0, i], partner))
            mine = pltpu.make_async_copy(source, place, local.at[i])
            mine.start()
            own.append(mine)
        for k in range(1, chips):
            origin = lax.rem(y - k + chips, chips) * 2 + c
            far_copies[k, 0].wait_recv()
            far_copies[k, 1].wait_recv()
            block = o_ref.at[:, origin]
            core.append(send(block, block, core_s.at[k, 0], core_r.at[k, 0], partner))
        for copy in far_copies.values():
            copy.wait_send()
        for copy in core + own:
            copy.wait()

    dma = pltpu.SemaphoreType.DMA
    return call(
        kernel,
        jax.ShapeDtypeStruct((pair, ten, rows, width), prefix.dtype),
        [dma((chips, 2))] * 4 + [dma((2,))],
        collective_id,
        [prefix, fresh],
    )


def swap_columns(x, collective_id):
    ten = lax.axis_size("ten")
    rows, columns = x.shape
    width = columns // ten

    def kernel(x_ref, o_ref, s_sem, r_sem, local):
        t = lax.axis_index("ten")
        peers = [lax.rem(t + k, ten) for k in range(1, ten)]
        greet([{"ten": p} for p in peers])

        def part(p):
            return x_ref.at[:, pl.ds(pl.multiple_of(p * width, 128), width)]

        copies = [
            send(part(p), o_ref.at[t], s_sem.at[k], r_sem.at[k], {"ten": p})
            for k, p in enumerate(peers)
        ]
        own = pltpu.make_async_copy(part(t), o_ref.at[t], local)
        own.start()
        own.wait()
        for copy in copies:
            copy.wait()

    dma = pltpu.SemaphoreType.DMA
    return call(
        kernel,
        jax.ShapeDtypeStruct((ten, rows, width), x.dtype),
        [dma((ten - 1,)), dma((ten - 1,)), dma],
        collective_id,
        [x],
    )


def scatter_sum(x, collective_id):
    ten, rows, columns = x.shape
    chips = ten // 2

    def kernel(x_ref, o_ref, near, pair, landed, core_s, core_r, far_s, far_r):
        t, y, c = coords()
        partner = {"ten": y * 2 + 1 - c}
        order = [lax.rem(y + k, chips) for k in range(chips)]
        greet([{"ten": order[k] * 2 + c} for k in range(1, chips)] + [partner])
        sequence = list(range(1, chips)) + [0]
        core = {}
        for k in sequence:
            core[k] = send(
                x_ref.at[order[k] * 2 + 1 - c], near.at[k], core_s.at[k], core_r.at[k], partner
            )
        far = []
        for k in sequence:
            core[k].wait_recv()
            total = x_ref[order[k] * 2 + c].astype(jnp.float32) + near[k].astype(jnp.float32)
            if k:
                pair[k] = total.astype(pair.dtype)
                far.append(
                    send(
                        pair.at[k],
                        landed.at[k],
                        far_s.at[k],
                        far_r.at[k],
                        {"ten": order[k] * 2 + c},
                    )
                )
            else:
                o_ref[...] = total
        for k, copy in enumerate(far, 1):
            copy.wait_recv()
            o_ref[...] += landed[k].astype(jnp.float32)
        for copy in far + list(core.values()):
            copy.wait_send()

    dma = pltpu.SemaphoreType.DMA
    buffer = pltpu.VMEM((chips, rows, columns), x.dtype)
    return call(
        kernel,
        jax.ShapeDtypeStruct((rows, columns), jnp.float32),
        [buffer] * 3 + [dma((chips,))] * 4,
        collective_id,
        [x],
    )


def expert_layer(x, w_gate, w_up, w_down, collective_id):
    groups, local, slots, width = x.shape
    hidden_units = w_gate.shape[2]
    ten = lax.axis_size("ten")
    chips = ten // 2
    piece = 256 if hidden_units % 256 == 0 else hidden_units
    pieces = hidden_units // piece
    stages = local * pieces
    rows = ten * groups * slots
    depth = min(stages, max(2, (38 << 20) // (6 * width * piece) if rows < 512 else 2))

    def kernel(
        x_ref, wg, wu, wd, o_ref,
        gbuf, ubuf, dbuf, arrived, xs, acc, part, near, pair, landed, ready,
        w_sem, own_sem, z_s, z_r, y_s, y_r, c_s, c_r, rc_s, rc_r, ry_s, ry_r, rz_s, rz_r,
    ):
        t, y, c = coords()
        g = lax.axis_index("exp")
        partner = {"ten": y * 2 + 1 - c}
        order = [lax.rem(g + k, groups) for k in range(groups)]
        origin = [lax.rem(g - k + groups, groups) for k in range(groups)]
        ahead = [lax.rem(y + j, chips) for j in range(chips)]
        behind = [lax.rem(y - j + chips, chips) * 2 + c for j in range(chips)]
        far = [{"ten": ahead[j] * 2 + c} for j in range(chips)]
        sequence = list(range(1, groups)) + [0]
        inner = list(range(1, chips)) + [0]

        def remote(src, dst, send_sem, recv_sem, peer):
            return pltpu.make_async_remote_copy(
                src_ref=src,
                dst_ref=dst,
                send_sem=send_sem,
                recv_sem=recv_sem,
                device_id=peer,
                device_id_type=MESH,
            )

        def weights(s):
            l, f, slot = s // pieces, lax.rem(s, pieces), lax.rem(s, depth)
            span = pl.ds(pl.multiple_of(f * piece, piece), piece)
            return [
                pltpu.make_async_copy(wg.at[l, :, span], gbuf.at[slot], w_sem.at[slot, 0]),
                pltpu.make_async_copy(wu.at[l, :, span], ubuf.at[slot], w_sem.at[slot, 1]),
                pltpu.make_async_copy(wd.at[l, span, :], dbuf.at[slot], w_sem.at[slot, 2]),
            ]

        def own_copy(l):
            return pltpu.make_async_copy(x_ref.at[g, l], arrived.at[l, t, g], own_sem.at[l])

        def z_copy(l, k):
            return remote(
                x_ref.at[order[k], l], arrived.at[l, t, g], z_s.at[l, k], z_r.at[l, k],
                {"exp": order[k]},
            )

        def y_copy(l, k, j):
            block = arrived.at[l, t, origin[k]]
            source = block if k else x_ref.at[g, l]
            return remote(source, block, y_s.at[l, k, j], y_r.at[l, k, j], far[j])

        def c_copy(l, k, j):
            block = arrived.at[l, behind[j], origin[k]]
            source = block if k or j else x_ref.at[g, l]
            return remote(source, block, c_s.at[l, k, j], c_r.at[l, k, j], partner)

        def rc_copy(l, k, j):
            return remote(
                part.at[l, ahead[j] * 2 + 1 - c, order[k]], near.at[l, k, j],
                rc_s.at[l, k, j], rc_r.at[l, k, j], partner,
            )

        def ry_copy(l, k, j):
            return remote(
                pair.at[l, k, j], landed.at[l, k, j], ry_s.at[l, k, j], ry_r.at[l, k, j], far[j]
            )

        def rz_copy(l, k):
            return remote(
                ready.at[l, k], o_ref.at[g, l], rz_s.at[l, k], rz_r.at[l, k], {"exp": order[k]}
            )

        def forward(l):
            for k in range(groups):
                for j in range(1, chips):
                    y_copy(l, k, j).wait_recv()
                    c_copy(l, k, j).start()

        def summed(l, k, j):
            rc_copy(l, k, j).wait_recv()
            mine = part[l, ahead[j] * 2 + c, order[k]].astype(jnp.float32)
            return mine + near[l, k, j].astype(jnp.float32)

        def sum_across(l):
            for k in sequence:
                for j in range(1, chips):
                    pair[l, k, j] = summed(l, k, j).astype(pair.dtype)
                    ry_copy(l, k, j).start()

        def send_back(l):
            for k in sequence:
                total = summed(l, k, 0)
                for j in range(1, chips):
                    ry_copy(l, k, j).wait_recv()
                    total = total + landed[l, k, j].astype(jnp.float32)
                if k:
                    ready[l, k] = total.astype(ready.dtype)
                    rz_copy(l, k).start()
                else:
                    o_ref[g, l] = total.astype(o_ref.dtype)

        for s in range(depth):
            for copy in weights(s):
                copy.start()
        greet([{"exp": order[k]} for k in range(1, groups)] + far[1:] + [partner])
        for l in range(local):
            for k in range(1, groups):
                z_copy(l, k).start()
            own_copy(l).start()
        for l in range(local):
            for k in range(groups):
                if k:
                    z_copy(l, k).wait_recv()
                for j in range(1, chips):
                    y_copy(l, k, j).start()
                c_copy(l, k, 0).start()
        forward(0)

        @pl.loop(0, stages)
        def _(s):
            l, f, slot = s // pieces, lax.rem(s, pieces), lax.rem(s, depth)

            @pl.when(f == 0)
            def _():
                own_copy(l).wait()
                for k in range(groups):
                    for j in range(chips):
                        c_copy(l, k, j).wait_recv()
                rows_in = arrived[l].astype(jnp.float32)
                xs[...] = rows_in.reshape(rows, width).astype(xs.dtype)
                acc[...] = jnp.zeros_like(acc)

            @pl.when((f == min(2, pieces - 1)) & (l + 1 < local))
            def _():
                forward(l + 1)

            for copy in weights(s):
                copy.wait()
            tokens = xs[...]
            gate = jnp.dot(tokens, gbuf[slot], preferred_element_type=jnp.float32)
            up = jnp.dot(tokens, ubuf[slot], preferred_element_type=jnp.float32)
            hidden = (gate / (1.0 + jnp.exp(-gate)) * up).astype(jnp.bfloat16)
            acc[...] += jnp.dot(hidden, dbuf[slot], preferred_element_type=jnp.float32)

            @pl.when(s + depth < stages)
            def _():
                for copy in weights(s + depth):
                    copy.start()

            @pl.when((f == min(2, pieces - 1)) & (l > 0))
            def _():
                sum_across(l - 1)

            @pl.when((f == min(5, pieces - 1)) & (l > 0))
            def _():
                send_back(l - 1)

            @pl.when(f == pieces - 1)
            def _():
                part[l] = acc[...].reshape(ten, groups, slots, width).astype(part.dtype)
                for k in sequence:
                    for j in inner:
                        rc_copy(l, k, j).start()

        sum_across(local - 1)
        send_back(local - 1)
        for l in range(local):
            for k in range(groups):
                if k:
                    z_copy(l, k).wait_send()
                    rz_copy(l, k).wait()
                for j in range(chips):
                    c_copy(l, k, j).wait_send()
                    rc_copy(l, k, j).wait_send()
                    if j:
                        y_copy(l, k, j).wait_send()
                        ry_copy(l, k, j).wait_send()

    dma = pltpu.SemaphoreType.DMA
    whole = pltpu.VMEM((local, ten, groups, slots, width), x.dtype)
    half = pltpu.VMEM((local, groups, chips, slots, width), x.dtype)
    across, along = dma((local, groups)), dma((local, groups, chips))
    hbm = pl.BlockSpec(memory_space=pl.ANY)
    return pl.pallas_call(
        kernel,
        out_shape=jax.ShapeDtypeStruct(x.shape, x.dtype),
        in_specs=[VMEM, hbm, hbm, hbm],
        out_specs=VMEM,
        scratch_shapes=[
            pltpu.VMEM((depth, width, piece), x.dtype),
            pltpu.VMEM((depth, width, piece), x.dtype),
            pltpu.VMEM((depth, piece, width), x.dtype),
            whole,
            pltpu.VMEM((rows, width), x.dtype),
            pltpu.VMEM((rows, width), jnp.float32),
            whole,
            half,
            half,
            half,
            pltpu.VMEM((local, groups, slots, width), x.dtype),
            dma((depth, 3)),
            dma((local,)),
            across, across, along, along, along, along, along, along, along, along, across, across,
        ],
        compiler_params=pltpu.CompilerParams(
            collective_id=collective_id, has_side_effects=True, vmem_limit_bytes=67043328
        ),
    )(x, w_gate, w_up, w_down)


def on_device(
    hidden_in,
    queries,
    new_kv,
    prefix_kv,
    decode_kv,
    prefix_len,
    decode_len,
    out_proj,
    norm_gain,
    router_w,
    expert_ids,
    w_gate,
    w_up,
    w_down,
):
    ten_size = lax.axis_size("ten")
    groups = lax.axis_size("exp")
    my_ten = lax.axis_index("ten")
    rows_dev, model_width = hidden_in.shape
    dec_dev = decode_len.shape[0]
    span_dev = rows_dev - dec_dev
    kv_width = new_kv.shape[2]
    heads_kv = kv_width // HD
    heads_q = queries.shape[1] // HD
    per_kv = heads_q // heads_kv
    score_scale = HD ** (-0.5)
    ctx_len = decode_kv.shape[2]
    own_heads = queries.reshape(rows_dev, heads_kv, per_kv, HD)
    dec_keys = jnp.concatenate([decode_kv[0], new_kv[0, span_dev:, None]], axis=1).reshape(
        dec_dev, ctx_len + 1, heads_kv, HD
    )
    dec_values = jnp.concatenate([decode_kv[1], new_kv[1, span_dev:, None]], axis=1).reshape(
        dec_dev, ctx_len + 1, heads_kv, HD
    )
    dec_scores = (
        jnp.einsum(
            "dcgh,dpch->dcgp", own_heads[span_dev:], dec_keys, preferred_element_type=jnp.float32
        )
        * score_scale
    )
    dec_pos = jnp.arange(ctx_len + 1, dtype=jnp.int32)[None, :]
    dec_visible = ((dec_pos < decode_len[:, None]) | (dec_pos == ctx_len))[:, None, None, :]
    dec_max, dec_exponent, dec_totals = local_softmax(dec_scores, dec_visible)
    dec_partial = jnp.einsum(
        "dcgp,dpch->dcgh",
        dec_exponent.astype(jnp.bfloat16),
        dec_values,
        preferred_element_type=jnp.float32,
    )
    cached = prefix_kv.shape[2]
    block_rows = cached + rows_dev
    both = gather_cache(prefix_kv[:, 0], new_kv, 0)
    both = both.reshape(2, ten_size * block_rows, heads_kv, HD)
    key_rows, value_rows = both[0], both[1]
    scores = (
        jnp.einsum(
            "rcgh,pch->rcgp", own_heads[:span_dev], key_rows, preferred_element_type=jnp.float32
        )
        * score_scale
    )
    query_row = my_ten * span_dev + jnp.arange(span_dev, dtype=jnp.int32)[:, None]
    place = jnp.arange(ten_size * block_rows, dtype=jnp.int32)[None, :]
    owner, offset = place // block_rows, place % block_rows
    fresh = offset - cached
    visible = jnp.where(
        fresh < 0,
        owner * cached + offset < prefix_len[0],
        (fresh < span_dev) & (owner * span_dev + fresh <= query_row),
    )[:, None, None, :]
    row_max, exponent, totals = local_softmax(scores, visible)
    span_out = (
        jnp.einsum(
            "rcgp,pch->rcgh",
            exponent.astype(jnp.bfloat16),
            value_rows,
            preferred_element_type=jnp.float32,
        )
        / totals[..., None]
    )
    dec_out = dec_partial / dec_totals[..., None]
    attended_rows = (
        jnp.concatenate([span_out, dec_out], axis=0)
        .reshape(rows_dev, heads_q * HD)
        .astype(jnp.bfloat16)
    )
    row_block = swap_columns(attended_rows, 1).reshape(ten_size * rows_dev, -1)
    shares = jnp.dot(row_block, out_proj, preferred_element_type=jnp.float32).astype(jnp.bfloat16)
    projected = scatter_sum(shares.reshape(ten_size, rows_dev, model_width), 2)
    residual = hidden_in.astype(jnp.float32) + projected
    mean_square = jnp.mean(residual * residual, axis=1, keepdims=True)
    normed = (residual * lax.rsqrt(mean_square + 1e-05) * norm_gain).astype(jnp.bfloat16)
    logits = jnp.dot(normed, router_w, preferred_element_type=jnp.float32)
    experts = router_w.shape[1]
    chosen_hot = (expert_ids[:, :, None] == jnp.arange(experts, dtype=jnp.int32)).astype(jnp.int32)
    chosen_logits = jnp.sum(jnp.where(chosen_hot == 1, logits[:, None, :], 0.0), axis=2)
    route_weights = jax.nn.softmax(chosen_logits, axis=1)
    flat_hot = chosen_hot.reshape(rows_dev * 2, experts)
    slot_rank = jnp.sum((jnp.cumsum(flat_hot, axis=0) - flat_hot) * flat_hot, axis=1).reshape(
        rows_dev, 2
    )
    capacity = SLOTS
    slot_index = jnp.arange(capacity, dtype=jnp.int32)
    assignment = chosen_hot[:, :, :, None] * (slot_rank[:, :, None, None] == slot_index).astype(
        jnp.int32
    )
    placement = jnp.sum(assignment, axis=1)
    local_experts = experts // groups
    placement_split = placement.reshape(rows_dev, groups, local_experts, capacity).astype(
        jnp.bfloat16
    )
    outgoing = jnp.einsum(
        "rnlc,rd->nlcd", placement_split, normed, preferred_element_type=jnp.float32
    ).astype(jnp.bfloat16)
    returned = expert_layer(outgoing, w_gate, w_up, w_down, 3)
    outputs = returned.reshape(experts * capacity, model_width).astype(jnp.float32)
    weight_map = jnp.sum(
        assignment.astype(jnp.float32) * route_weights[:, :, None, None], axis=1
    ).reshape(rows_dev, experts * capacity)
    expert_mix = jnp.dot(
        weight_map, outputs, precision=lax.Precision.HIGHEST, preferred_element_type=jnp.float32
    )
    return (residual + expert_mix).astype(jnp.bfloat16)


def solution(mesh):
    in_specs = (
        P(("rep", "exp", "ten"), None),
        P(("rep", "exp", "ten"), None),
        P(None, ("rep", "exp", "ten"), None),
        P(None, ("rep", "exp"), "ten", None),
        P(None, ("rep", "exp", "ten"), None, None),
        P(("rep", "exp")),
        P(("rep", "exp", "ten")),
        P("ten", None),
        P(),
        P(),
        P(("rep", "exp", "ten"), None),
        P("exp", None, "ten"),
        P("exp", None, "ten"),
        P("exp", "ten", None),
    )
    out_specs = P(("rep", "exp", "ten"), None)
    return jax.shard_map(
        on_device, mesh=mesh, in_specs=in_specs, out_specs=out_specs, check_vma=False
    )
```
